32 devices in a mesh: vocab: 8 (over z, y), feat: 4 (over x, core).
Axes of the slice: x: 2, y: 2, z: 4, core: 2. Of those that a mesh axis runs over, the one named last changes fastest.
Arguments:
- hidden: bfloat16 [1024, 4096], P('feat'), may hold values from -64 to 64
- out_head: bfloat16 [32768, 4096], P(('vocab', 'feat')), may hold values from -0.28125 to 0.28125
- out_proj: bfloat16 [32768, 128], P(('vocab', 'feat')), may hold values from -5 to 5
- in_proj: bfloat16 [4096, 128], replicated, may hold values from -0.09375 to 0.09375
- targets: int32 [1024], replicated, may hold values from 0 to 32767
- seq_ids: int32 [1024], replicated, may hold values from 0 to 15, never falling along the last dimension, each value on 1 to 128 neighbouring positions
- grad_store: bfloat16 [16384, 16384], P('vocab', 'feat'), may hold values from -0.01953125 to 0.01953125
Outputs:
- influence: float32 [16384, 16], P(('vocab', 'feat'))
The draws below stay inside these ranges and needn't reach their ends.
All inputs are finite; a program needn't handle non-finite values.
Results may differ from the reference program's by a relative error of at most 0.003.
Values may be sent and summed in bfloat16 or wider, within the bound.
A program may use at most 128 MiB of HBM per device.

```python
import math
import jax
import jax.numpy as jnp
import numpy as np
from jax import lax

D = 4096
R = 128
SEQS = 16
VOCAB = 32768
TOKENS = 1024
EXAMPLES = 16384
FEATS = 16384


def head_rows(key, row_ids):
    base_key = jax.random.fold_in(key, 7)

    def single(row_id):
        values = jax.random.normal(jax.random.fold_in(base_key, row_id), (D,), jnp.float32)
        return jnp.clip(values, -6.0, 6.0) * (3.0 / math.sqrt(D))
    return jax.vmap(single)(row_ids)


def draw_out_head(key, part):
    return head_rows(key, jnp.arange(VOCAB, dtype=jnp.int32)).astype(jnp.bfloat16)


def draw_hidden(key, part):
    values = jnp.clip(jax.random.normal(jax.random.fold_in(key, 3), (TOKENS, D), jnp.float32), -5.0, 5.0)
    return values.astype(jnp.bfloat16)


def place_ends(drawn, rng, low, high):
    longest = drawn.shape.index(max(drawn.shape))
    spots = []
    for shift in (0, 1):
        where = [jax.random.randint(jax.random.fold_in(rng, axis), (), 0, length) for axis, length in enumerate(drawn.shape)]
        where[longest] = (where[longest] + shift) % drawn.shape[longest]
        spots.append(tuple(where))
    return drawn.at[spots[0]].set(low).at[spots[1]].set(high)


def with_spikes(result, stream_key, source, target, blocks, factor):
    owner, partner = [(jnp.arange(result.shape[position]) // (result.shape[position] // blocks)).reshape([-1 if axis == position else 1 for axis in range(result.ndim)]) for position in (source, target)]
    chosen = jax.random.permutation(stream_key, blocks)[partner]
    strong = (owner == chosen) | (owner == (partner + blocks // 2) % blocks)
    return jnp.where(strong, factor * result, result)


def block_scale(own_key, shape, split, smallest, top_value):
    def one(position, parts):
        draws = jax.random.uniform(jax.random.fold_in(jax.random.fold_in(own_key, 6), position), (parts,), jnp.float32, smallest / len(split), top_value / len(split))
        return jnp.repeat(jnp.exp(draws), shape[position] // parts).reshape((-1,) + (1,) * (len(shape) - position - 1))

    level = one(*split[0])
    for cut in split[1:]:
        level = level * one(*cut)
    return level


def split_up(amount, total, most, lean):
    loads = [(1 << 20) // math.isqrt(standing ** lean) + 1 for standing in range(2, amount + 1)]
    spare, holding = total - most - (amount - 1), [1] * (amount - 1)
    while spare > 0:
        candidates = [i for i in range(amount - 1) if holding[i] < most]
        pool, remaining = sum([loads[i] for i in candidates]), spare
        for i in candidates:
            more = min(most - holding[i], max(1, remaining * loads[i] // pool), spare)
            holding[i] = holding[i] + more
            spare = spare - more
    return np.array([most] + holding)


def ragged_sizes(key, number_of, total, reach, lean):
    if number_of == 2:
        one = jax.random.randint(key, (), max(1, total - reach), min(reach, total - 1) + 1)
        return jnp.stack([one, total - one])
    sizes = jnp.asarray(split_up(number_of, total, reach, lean), jnp.int32)
    couples = (number_of - 1) // 2
    donor, sink = sizes[1:1 + 2 * couples:2], sizes[2:2 + 2 * couples:2]
    margin = jnp.minimum(donor - 1, reach - sink)
    moved = jax.random.randint(jax.random.fold_in(key, 1), (couples,), 0, 1 << 20) % (margin + 1)
    sizes = sizes.at[1:1 + 2 * couples:2].set(donor - moved).at[2:2 + 2 * couples:2].set(sink + moved)
    return sizes[jax.random.permutation(jax.random.fold_in(key, 2), number_of)]


def bell_draw(key, shape, scale, limit, cuts=(), kind=jnp.bfloat16):
    drawn = jax.random.normal(key, shape, jnp.float32) * scale
    if len(cuts) > 0:
        drawn = block_scale(key, shape, cuts, -0.22, 0.18) * drawn
    return jnp.clip(drawn, min=-limit, max=limit).astype(kind)


def gaussian_with(key, shape, width, bound, split, heavy, kind=jnp.bfloat16):
    entries = width * jax.random.normal(key, shape, jnp.float32)
    if split:
        entries = entries * block_scale(key, shape, split, -0.22, 0.18)
    return jnp.clip(with_spikes(entries, jax.random.fold_in(key, 3), *heavy), -bound, bound).astype(kind)


def setup_inputs(seed: int = 0) -> dict:
    keys = jax.random.split(jax.random.key(seed), 8)
    return {
        "hidden": draw_hidden(jax.random.fold_in(keys[7], 71), 0),
        "out_head": draw_out_head(jax.random.fold_in(keys[7], 71), 0),
        "out_proj": bell_draw(keys[2], (VOCAB, R), 1.0, 5.0, ((0, 32),)),
        "in_proj": bell_draw(keys[3], (D, R), D ** -0.5, 0.09375),
        "targets": place_ends(jax.random.randint(keys[4], (TOKENS,), 0, VOCAB), jax.random.fold_in(keys[4], 1), 0, VOCAB - 1).astype(jnp.int32),
        "seq_ids": jnp.searchsorted(jnp.cumsum(ragged_sizes(keys[5], SEQS, TOKENS, 2 * TOKENS // SEQS, 0)), jnp.arange(TOKENS), side="right").astype(jnp.int32),
        "grad_store": gaussian_with(keys[6], (EXAMPLES, FEATS), (1.0 / (8.0 * R)), 0.01953125, ((0, 8), (1, 4)), (1, 0, 8, 2.0)),
    }


def reference(hidden, out_head, out_proj, in_proj, targets, seq_ids, grad_store):
    logits = jnp.dot(hidden, out_head.T, preferred_element_type=jnp.float32)
    row_max = jnp.max(logits, axis=1, keepdims=True)
    expval = jnp.exp(logits - row_max)
    row_sum = jnp.sum(expval, axis=1, keepdims=True)
    columns = jnp.arange(VOCAB, dtype=jnp.int32)
    onehot = (targets[:, None] == columns[None, :]).astype(jnp.float32)
    residual = (expval / row_sum - onehot).astype(jnp.bfloat16)
    out_side = jnp.dot(residual, out_proj, preferred_element_type=jnp.float32)
    in_side = jnp.dot(hidden, in_proj, preferred_element_type=jnp.float32)
    member = (seq_ids[:, None] == jnp.arange(SEQS, dtype=jnp.int32)[None, :]).astype(jnp.float32)
    query_grads = jnp.einsum("ts,ti,tj->sij", member, out_side, in_side, precision=lax.Precision.HIGHEST)
    query_grads = query_grads.reshape(SEQS, R * R).astype(jnp.bfloat16)
    return jnp.dot(grad_store, query_grads.T, preferred_element_type=jnp.float32)
```

```python
import functools

import jax
import jax.numpy as jnp
from jax import lax
from jax.experimental import pallas as pl
from jax.experimental.pallas import tpu as pltpu
from jax.sharding import PartitionSpec as P

SEQS = 16
SUBS = 8
F32 = jnp.float32
BF16 = jnp.bfloat16
NT = (((1,), (1,)), ((), ()))


def kernel(nv, nf, hid_in, head_in, oproj_in, iproj_in, targets_in, seqs_in, gs_in, out,
           hid, head, oproj, iproj, targets, seqs, gs, lg, o_t, o_full, ins, sv, so, s2, st, rv, r0, r1, ro, rst, osb,
           qg, qgm, part, infl,
           load_sem, x_send, y_send, z_send, s_send, own_send, recv, s_recv, own_recv, so_sem, ox_send, ox_recv, ro_sem,
           sv_sem, st_sem, ag_send, ag_recv, in_sem, loc_sem, heard):
    v = lax.axis_index("vocab")
    f = lax.axis_index("feat")
    me = v * nf + f
    nd = nv * nf
    x, k = f // 2, f % 2
    xn = nf // 2
    sib = f + 1 - 2 * k
    vy = v + 1 - 2 * (v % 2)
    vz = v + 2 - 4 * ((v // 2) % 2)
    vd = vy + vz - v
    vl = head.shape[0]
    width = head.shape[1]
    rank = oproj.shape[1]
    rf, tb = sv.shape[1], sv.shape[2]
    parts = hid.shape[1]
    tc = 2 * tb
    eo = out.shape[1]
    piece = tb // 4
    per = SUBS // parts
    sr = 2 * piece // per
    quarter = nv // 4

    def owner(h, i):
        spot = (1 - i % 2) * (i // 2) + (i % 2) * (2 * quarter - 1 - i // 2)
        return quarter + spot if h else spot + 2 * quarter * (spot // quarter)

    def block(w):
        late = ((w // quarter + 1) // 2) % 2
        spot = late * (w - quarter) + (1 - late) * (w - 2 * quarter * (w // (2 * quarter)))
        i = (1 - spot // quarter) * 2 * spot + (spot // quarter) * (4 * quarter - 1 - 2 * spot)
        return 2 * i + late

    mb = block(v)

    loads = [
        pltpu.make_async_copy(oproj_in, oproj, load_sem.at[0]),
        pltpu.make_async_copy(targets_in, targets, load_sem.at[1]),
        pltpu.make_async_copy(head_in, head, load_sem.at[2]),
        pltpu.make_async_copy(iproj_in, iproj, load_sem.at[3]),
        pltpu.make_async_copy(seqs_in, seqs, load_sem.at[4]),
        pltpu.make_async_copy(gs_in, gs, load_sem.at[5]),
    ]

    def half(xi, kk, h):
        return hid.at[xi, h, pl.ds(pl.multiple_of(kk * tb, tb), tb)]

    mine = [pltpu.make_async_copy(hid_in.at[pl.ds(h * tb, tb)], half(x, k, h), load_sem.at[6 + h])
            for h in range(parts)]

    def flip(i, bit):
        return i + bit - 2 * bit * ((i // bit) % 2)

    near = [(v, flip(f, 1 << i)) for i in range(nf.bit_length() - 1)]
    near += [(flip(v, 1 << i), f) for i in range(nv.bit_length() - 1)]
    barrier = pltpu.get_barrier_semaphore()

    def signal(sem, place):
        pl.semaphore_signal(sem, inc=1, device_id={"vocab": place[0], "feat": place[1]},
                            device_id_type=pl.DeviceIdType.MESH)

    for place in near:
        signal(barrier, place)
    for copy in mine + loads[:5]:
        copy.start()
    with jax.named_scope("barrier"):
        pl.semaphore_wait(barrier, len(near))
    said = [0]

    def hear(upto):
        for i in range(said[0], upto):
            pl.semaphore_wait(heard.at[i], 1)
            if i + 1 < len(near):
                signal(heard.at[i + 1], near[i + 1])
        said[0] = max(said[0], upto)

    signal(heard.at[0], near[0])
    if xn > 2:
        hear(nf.bit_length() - 1)

    def remote(src, dst, ss, rs, dv, df):
        return pltpu.make_async_remote_copy(
            src_ref=src, dst_ref=dst, send_sem=ss, recv_sem=rs,
            device_id={"vocab": dv, "feat": df}, device_id_type=pl.DeviceIdType.MESH)

    def rows(xi, kk, own, j):
        c = j % per
        at = kk * tb + (own % 4) * piece + (c // 2) * sr
        cols = pl.ds((c % 2) * (width // 2), width // 2)
        return hid.at[xi, j // per, pl.ds(pl.multiple_of(at, sr), sr), cols]

    for h in range(parts):
        mine[h].wait()
        for r in range(xn - 1):
            fo = 2 * ((x + r + 1) % xn) + k
            for j in range(h * per, (h + 1) * per):
                blk = rows(x, k, v, j)
                remote(blk, blk, x_send.at[r], recv.at[r, 0, j], v, fo).start()
        if h == parts - 1:
            for r in range(xn - 1):
                fo = 2 * ((x + r + 1) % xn) + k
                for j in range(h * per, (h + 1) * per):
                    blk = rows(x, k, vd, j)
                    remote(blk, blk, x_send.at[r], recv.at[r, 3, j], v, fo).start()
        remote(half(x, k, h), half(x, k, h), own_send, own_recv.at[h], v, sib).start()
    loads[5].start()

    def src_of(r):
        return (x + xn - r - 1) % xn

    owners = (v, vy, vz, vd)

    def arrive(r, rel, j):
        blk = rows(src_of(r), k, owners[rel], j)
        remote(blk, blk, x_send.at[r], recv.at[r, rel, j], v, f).wait_recv()
        relay = j // per < parts - 1
        if rel == 0:
            remote(blk, blk, y_send.at[r], recv.at[r, 1, j], vy, f).start()
            remote(blk, blk, z_send.at[r], recv.at[r, 2, j], vz, f).start()
        if rel == 1 and relay and j % 2 == 0:
            remote(blk, blk, z_send.at[r], recv.at[r, 3, j], vz, f).start()
        if rel == 2 and relay and j % 2 == 1:
            remote(blk, blk, y_send.at[r], recv.at[r, 3, j], vy, f).start()
        remote(blk, blk, s_send.at[r], s_recv.at[r, j // per], v, sib).start()

    def post(send_buf, recv_buf, sem, d):
        @pl.when(d != me)
        def _():
            remote(send_buf, recv_buf, sem.at[0], sem.at[1], d // nf, d % nf).start()

    hear(1)
    loads[0].wait()
    loads[1].wait()
    o_t[...] = oproj[...].astype(F32).T.astype(BF16)
    base = me * vl

    def onehot_step(c, carry):
        xi, h = c // parts, c % parts
        blks = [(2 * xi + kk) * parts + h for kk in range(2)]
        ids = lax.broadcasted_iota(jnp.int32, (vl, tc), 0) + base
        goal = jnp.concatenate([targets[b] for b in blks], axis=1)
        hot = (goal == ids).astype(F32).astype(BF16)
        o = jnp.dot(o_t[...], hot, preferred_element_type=F32)
        o_full[c] = o
        for kk in range(2):
            for g in range(nf):
                so[g % 2, g // 2, blks[kk]] = o[g * rf:(g + 1) * rf, kk * tb:(kk + 1) * tb].astype(BF16)
        return carry

    with jax.named_scope("onehot"):
        lax.fori_loop(0, xn * parts, onehot_step, 0)
    over = remote(so.at[1 - k], r0, so_sem.at[0], so_sem.at[1], v, sib)
    over.start()

    def across(p, g):
        return remote(r0.at[g], r1.at[p - 1], ox_send.at[p - 1], ox_recv.at[p - 1], v, 2 * g + k)

    def onehot_over():
        over.wait_recv()

        def one(b, c):
            for g in range(xn):
                r0[g, b] = r0[g, b] + so[k, g, b]
            return c

        lax.fori_loop(0, nv, one, 0)
        for p in range(1, xn):
            across(p, (x + p) % xn).start()

    def spread_to(p):
        b = block((v + p) % nv)
        return remote(s2.at[b], ro.at[p - 1], ro_sem.at[0], ro_sem.at[1], (v + p) % nv, f)

    def onehot_sum():
        for p in range(1, xn):
            across(p, x).wait_recv()

        def one(b, c):
            t = r0[x, b]
            for p in range(1, xn):
                t = t + r1[p - 1, b]
            s2[b] = t
            return c

        lax.fori_loop(0, nv, one, 0)
        for p in range(1, nv):
            spread_to(p).start()

    def tiles(xi, h, lo, hi, m):
        vt = (hi - lo) // 2

        def tile(i, m):
            at = pl.ds(pl.multiple_of(i * vt, vt), vt)
            l = lax.dot_general(head[at, :], hid[xi, h], NT, preferred_element_type=F32)
            lg[at, :] = l
            return jnp.maximum(m, jnp.max(l, axis=0, keepdims=True))

        with jax.named_scope("tiles"):
            return lax.fori_loop(lo // vt, hi // vt, tile, m)

    def finish(xi, h, m):
        with jax.named_scope("finish"):
            e = jnp.exp(lg[...] - m)
            s = jnp.sum(e, axis=0, keepdims=True)
            u = jnp.dot(o_t[...], e.astype(BF16), preferred_element_type=F32)
            u = u / s - o_full[xi * parts + h]
            own = [owner(h, 2 * xi + kk) for kk in range(2)]
            for kk in range(2):
                lanes = slice(kk * tb, (kk + 1) * tb)
                st[own[kk], 0:1, :] = m[:, lanes]
                st[own[kk], 1:2, :] = s[:, lanes]
                for g in range(nf):
                    sv[own[kk] * nf + g] = u[g * rf:(g + 1) * rf, lanes].astype(BF16)
            for kk in range(2):
                for g in range(nf):
                    d = own[kk] * nf + g
                    post(st.at[own[kk]], rst.at[me], st_sem, d)
                    post(sv.at[d], rv.at[me], sv_sem, d)

    def project(xi, h):
        with jax.named_scope("act"):
            act = jnp.dot(hid[xi, h], iproj[...], preferred_element_type=F32)
            hi = act.astype(BF16)
            lo = (act - hi.astype(F32)).astype(BF16)
            both = jnp.concatenate([hi, lo], axis=1)
            for kk in range(2):
                ins[(2 * xi + kk) * parts + h] = both[kk * tb:(kk + 1) * tb]

    low = jnp.full((1, tc), -jnp.inf, F32)
    every = range(xn - 1)

    def sibling(h):
        blk = half(x, 1 - k, h)
        remote(blk, blk, own_send, own_recv.at[h], v, sib).wait_recv()

    def arrivals(*which):
        with jax.named_scope("arr"):
            for rel, j in which:
                for r in every:
                    arrive(r, rel, j)

    def passed(r, h):
        with jax.named_scope("passed"):
            blk = half(src_of(r), 1 - k, h)
            remote(blk, blk, s_send.at[r], s_recv.at[r, h], v, sib).wait_recv()

    mid = vl // 2
    hear(2)
    loads[2].wait()
    loads[3].wait()
    sibling(0)
    m = tiles(x, 0, 0, mid, low)
    hear(3)
    arrivals((0, 0))
    hear(4)
    m = tiles(x, 0, mid, vl, m)
    arrivals((0, 1))
    with jax.named_scope("hear"):
        hear(len(near))
    finish(x, 0, m)
    arrivals((0, 2), (1, 0), (2, 0))
    sibling(1)
    m = tiles(x, 1, 0, mid, low)
    arrivals((0, 3), (1, 1), (2, 1))
    m = tiles(x, 1, mid, vl, m)
    arrivals((0, 4), (1, 2), (2, 2))
    finish(x, 1, m)
    arrivals((0, 5), (1, 3), (2, 3))
    project(x, 0)
    arrivals((0, 6), (1, 4), (2, 4))
    with jax.named_scope("over"):
        onehot_over()
    arrivals((0, 7), (1, 5), (2, 5), (3, 0), (3, 1))
    project(x, 1)
    arrivals((3, 2), (3, 4), (3, 3))
    for r in every:
        passed(r, 0)
        m = tiles(src_of(r), 0, 0, mid, low)
        if r == 0:
            arrivals((3, 5), (1, 6), (2, 6))
        m = tiles(src_of(r), 0, mid, vl, m)
        if r == 0:
            arrivals((3, 6))
        finish(src_of(r), 0, m)
    arrivals((3, 7), (1, 7), (2, 7))
    for r in every:
        project(src_of(r), 0)
    with jax.named_scope("ohsum"):
        onehot_sum()
    for r in every:
        passed(r, 1)
        finish(src_of(r), 1, tiles(src_of(r), 1, 0, vl, low))
    for r in every:
        project(src_of(r), 1)

    local = [pltpu.make_async_copy(sv.at[me], rv.at[me], loc_sem.at[0]),
             pltpu.make_async_copy(st.at[v], rst.at[me], loc_sem.at[1])]
    for copy in local:
        copy.start()
    loads[4].wait()
    some = ro.at[pl.ds(0, nv - 1)]
    with jax.named_scope("row"):
        remote(some, some, ro_sem.at[0], ro_sem.at[1], v, f).wait_recv()
    targeted = s2[mb].astype(F32)
    for p in range(1, nv):
        targeted = targeted + ro[p - 1].astype(F32)
    for copy in local:
        copy.wait()
    stats, shares = rst.at[pl.ds(0, nd - 1)], rv.at[pl.ds(0, nd - 1)]
    with jax.named_scope("take"):
        remote(stats, stats, st_sem.at[0], st_sem.at[1], v, f).wait_recv()
        remote(shares, shares, sv_sem.at[0], sv_sem.at[1], v, f).wait_recv()
    peak, mass = rst[:, 0, :], rst[:, 1, :]
    mass = jnp.exp(peak - jnp.max(peak, axis=0, keepdims=True)) * mass
    share = mass / jnp.sum(mass, axis=0, keepdims=True)
    first_row = lax.broadcasted_iota(jnp.int32, (nd, tb), 0) * vl
    goal = targets[mb]
    outside = (goal < first_row) | (goal >= first_row + vl)
    acc = -jnp.sum(jnp.where(outside, share, 0.0), axis=0, keepdims=True) * targeted
    for d in range(nd):
        w = share[d:d + 1, :]
        acc = acc + w * rv[d].astype(F32)
    osb[mb] = acc

    with jax.named_scope("spread"):
        for p in range(1, nv):
            remote(osb.at[mb], osb.at[mb], ag_send, ag_recv.at[v], (v + p) % nv, f).start()

    def outer(first, b1, b2):
        for b in (b1, b2):
            w = owner(b % 2, b // 2)

            @pl.when(v != w)
            def _():
                with jax.named_scope("agw"):
                    remote(osb.at[b], osb.at[b], ag_send, ag_recv.at[w], v, f).wait_recv()

        with jax.named_scope("outer"):
            member = jnp.concatenate([seqs[b1], seqs[b2]], axis=1) == lax.broadcasted_iota(jnp.int32, (SEQS, tc), 0)
            member = member.astype(F32)
            o = jnp.concatenate([osb[b1], osb[b2]], axis=1)
            hi = o.astype(BF16).astype(F32)
            lo = o - hi
            w_hi = jnp.concatenate([(member * hi[i:i + 1, :]).astype(BF16) for i in range(rf)], axis=0)
            w_lo = jnp.concatenate([(member * lo[i:i + 1, :]).astype(BF16) for i in range(rf)], axis=0)
            right = jnp.concatenate([ins[b1], ins[b2]], axis=0)
            t = jnp.dot(w_hi, right, preferred_element_type=F32)
            t = t[:, :rank] + t[:, rank:] + jnp.dot(w_lo, right[:, :rank], preferred_element_type=F32)
            qg[...] = t if first else qg[...] + t

    for b in range(0, nv, 4):
        outer(b == 0, b, b + 2)
    for b in range(1, nv, 4):
        outer(False, b, b + 2)
    for i in range(rf):
        qgm[:, i * rank:(i + 1) * rank] = qg[i * SEQS:(i + 1) * SEQS, :].astype(BF16)
    loads[5].wait()

    def score(p, c):
        t = p + 1
        g = 2 * ((x + t // 2) % xn) + (k + 1 + t % 2) % 2
        part[g] = lax.dot_general(
            qgm[...], gs[pl.ds(pl.multiple_of(g * eo, eo), eo), :], NT, preferred_element_type=F32)

        @pl.when(p < nf)
        def _():
            remote(part.at[g], infl.at[p - 1], in_sem.at[0], in_sem.at[1], v, g).start()
        return c

    with jax.named_scope("score"):
        lax.fori_loop(1, nf + 1, score, 0)
    result = part[f]
    with jax.named_scope("inflw"):
        landed = infl.at[pl.ds(0, nf - 1)]
        remote(landed, landed, in_sem.at[0], in_sem.at[1], v, f).wait_recv()
    for p in range(1, nf):
        result = result + infl[p - 1]
    out[...] = result

    def sent(ref, sem):
        remote(ref, ref, sem, sem, v, f).wait_send()

    with jax.named_scope("drain"):
        chunk = sr // 2
        for r in every:
            sent(hid.at[0, 0, pl.ds(0, (SUBS + per) * chunk)], x_send.at[r])
            sent(hid.at[0, 0, pl.ds(0, (SUBS + per // 2) * chunk)], y_send.at[r])
            sent(hid.at[0, 0, pl.ds(0, (SUBS + per // 2) * chunk)], z_send.at[r])
            sent(hid.at[0, 0], s_send.at[r])
        sent(hid.at[0, 0], own_send)
        over.wait_send()
        for p in range(1, xn):
            across(p, x).wait_send()
        sent(some, ro_sem.at[0])
        sent(stats, st_sem.at[0])
        sent(shares, sv_sem.at[0])
        sent(osb.at[pl.ds(0, nv - 1)], ag_send)
        sent(landed, in_sem.at[0])


def solution(mesh):
    nv, nf = mesh.shape["vocab"], mesh.shape["feat"]
    nd = nv * nf
    xn = nf // 2

    def on_device(hidden, out_head, out_proj, in_proj, targets, seq_ids, grad_store):
        tl, width = hidden.shape
        vl, rank = out_proj.shape
        el, fl = grad_store.shape
        tokens = tl * nf
        rf, tb, eo = rank // nf, tokens // nv, el // nf
        parts = tl // tb
        any_spec = pl.BlockSpec(memory_space=pl.ANY)
        vmem = pl.BlockSpec(memory_space=pltpu.VMEM)
        dma = pltpu.SemaphoreType.DMA
        res = pl.pallas_call(
            functools.partial(kernel, nv, nf),
            out_shape=jax.ShapeDtypeStruct((SEQS, eo), F32),
            in_specs=[any_spec] * 7,
            out_specs=vmem,
            scratch_shapes=[
                pltpu.VMEM((xn, parts, 2 * tb, width), BF16),
                pltpu.VMEM((vl, width), BF16),
                pltpu.VMEM((vl, rank), BF16),
                pltpu.VMEM((width, rank), BF16),
                pltpu.VMEM((nv, 1, tb), jnp.int32),
                pltpu.VMEM((nv, 1, tb), jnp.int32),
                pltpu.VMEM((el, fl), BF16),
                pltpu.VMEM((vl, 2 * tb), F32),
                pltpu.VMEM((rank, vl), BF16),
                pltpu.VMEM((xn * parts, rank, 2 * tb), F32),
                pltpu.VMEM((nv, tb, 2 * rank), BF16),
                pltpu.VMEM((nd, rf, tb), BF16),
                pltpu.VMEM((2, xn, nv, rf, tb), BF16),
                pltpu.VMEM((nv, rf, tb), BF16),
                pltpu.VMEM((nv, 2, tb), F32),
                pltpu.VMEM((nd, rf, tb), BF16),
                pltpu.VMEM((xn, nv, rf, tb), BF16),
                pltpu.VMEM((xn - 1, nv, rf, tb), BF16),
                pltpu.VMEM((nv - 1, rf, tb), BF16),
                pltpu.VMEM((nd, 2, tb), F32),
                pltpu.VMEM((nv, rf, tb), F32),
                pltpu.VMEM((rf * SEQS, rank), F32),
                pltpu.VMEM((SEQS, fl), BF16),
                pltpu.VMEM((nf, SEQS, eo), F32),
                pltpu.VMEM((nf - 1, SEQS, eo), F32),
                dma((6 + parts,)),
                dma((xn - 1,)),
                dma((xn - 1,)),
                dma((xn - 1,)),
                dma((xn - 1,)),
                dma,
                dma((xn - 1, 4, SUBS)),
                dma((xn - 1, parts)),
                dma((parts,)),
                dma((2,)),
                dma((xn - 1,)),
                dma((xn - 1,)),
                dma((2,)),
                dma((2,)),
                dma((2,)),
                dma,
                dma((nv,)),
                dma((2,)),
                dma((2,)),
                pltpu.SemaphoreType.REGULAR((nf.bit_length() + nv.bit_length() - 2,)),
            ],
            compiler_params=pltpu.CompilerParams(
                collective_id=0, has_side_effects=True, vmem_limit_bytes=60 * 1024 * 1024),
        )(hidden, out_head, out_proj, in_proj, targets.reshape(nv, 1, tb), seq_ids.reshape(nv, 1, tb), grad_store)
        return res.T

    in_specs = (
        P("feat", None),
        P(("vocab", "feat"), None),
        P(("vocab", "feat"), None),
        P(),
        P(),
        P(),
        P("vocab", "feat"),
    )
    return jax.shard_map(
        on_device, mesh=mesh, in_specs=in_specs, out_specs=P(("vocab", "feat"), None), check_vma=False
    )
```

```python
import functools

import jax
import jax.numpy as jnp
from jax import lax
from jax.experimental import pallas as pl
from jax.experimental.pallas import tpu as pltpu
from jax.sharding import PartitionSpec as P

SEQS = 16
SUBS = 8
F32 = jnp.float32
BF16 = jnp.bfloat16
NT = (((1,), (1,)), ((), ()))


def kernel(nv, nf, hid_in, head_in, oproj_in, iproj_in, targets_in, seqs_in, gs_in, out,
           hid, head, oproj, iproj, targets, seqs, gs, lg, o_t, o_full, ins, sv, so, s2, st, rv, r0, r1, ro, rst, osb,
           qg, qgm, part, infl,
           load_sem, x_send, y_send, z_send, s_send, own_send, recv, s_recv, own_recv, so_sem, ox_send, ox_recv, ro_sem,
           sv_sem, st_sem, ag_send, ag_recv, in_sem, loc_sem, heard):
    v = lax.axis_index("vocab")
    f = lax.axis_index("feat")
    me = v * nf + f
    nd = nv * nf
    x, k = f // 2, f % 2
    xn = nf // 2
    sib = f + 1 - 2 * k
    vy = v + 1 - 2 * (v % 2)
    vz = v + 2 - 4 * ((v // 2) % 2)
    vd = vy + vz - v
    vl = head.shape[0]
    width = head.shape[1]
    rank = oproj.shape[1]
    rf, tb = sv.shape[1], sv.shape[2]
    parts = hid.shape[1]
    tc = 2 * tb
    eo = out.shape[1]
    piece = tb // 4
    per = SUBS // parts
    sr = 2 * piece // per
    quarter = nv // 4

    def owner(h, i):
        spot = (1 - i % 2) * (i // 2) + (i % 2) * (2 * quarter - 1 - i // 2)
        return quarter + spot if h else spot + 2 * quarter * (spot // quarter)

    def block(w):
        late = ((w // quarter + 1) // 2) % 2
        spot = late * (w - quarter) + (1 - late) * (w - 2 * quarter * (w // (2 * quarter)))
        i = (1 - spot // quarter) * 2 * spot + (spot // quarter) * (4 * quarter - 1 - 2 * spot)
        return 2 * i + late

    mb = block(v)

    loads = [
        pltpu.make_async_copy(oproj_in, oproj, load_sem.at[0]),
        pltpu.make_async_copy(targets_in, targets, load_sem.at[1]),
        pltpu.make_async_copy(head_in, head, load_sem.at[2]),
        pltpu.make_async_copy(iproj_in, iproj, load_sem.at[3]),
        pltpu.make_async_copy(seqs_in, seqs, load_sem.at[4]),
        pltpu.make_async_copy(gs_in, gs, load_sem.at[5]),
    ]

    def half(xi, kk, h):
        return hid.at[xi, h, pl.ds(pl.multiple_of(kk * tb, tb), tb)]

    mine = [pltpu.make_async_copy(hid_in.at[pl.ds(h * tb, tb)], half(x, k, h), load_sem.at[6 + h])
            for h in range(parts)]

    def flip(i, bit):
        return i + bit - 2 * bit * ((i // bit) % 2)

    near = [(v, flip(f, 1 << i)) for i in range(nf.bit_length() - 1)]
    near += [(flip(v, 1 << i), f) for i in range(nv.bit_length() - 1)]
    barrier = pltpu.get_barrier_semaphore()

    def signal(sem, place):
        pl.semaphore_signal(sem, inc=1, device_id={"vocab": place[0], "feat": place[1]},
                            device_id_type=pl.DeviceIdType.MESH)

    for place in near:
        signal(barrier, place)
    for copy in mine + loads[:5]:
        copy.start()
    with jax.named_scope("barrier"):
        pl.semaphore_wait(barrier, len(near))
    said = [0]

    def hear(upto):
        for i in range(said[0], upto):
            pl.semaphore_wait(heard.at[i], 1)
            if i + 1 < len(near):
                signal(heard.at[i + 1], near[i + 1])
        said[0] = max(said[0], upto)

    signal(heard.at[0], near[0])
    if xn > 2:
        hear(nf.bit_length() - 1)

    def remote(src, dst, ss, rs, dv, df):
        return pltpu.make_async_remote_copy(
            src_ref=src, dst_ref=dst, send_sem=ss, recv_sem=rs,
            device_id={"vocab": dv, "feat": df}, device_id_type=pl.DeviceIdType.MESH)

    def rows(xi, kk, own, j):
        c = j % per
        at = kk * tb + (own % 4) * piece + (c // 2) * sr
        cols = pl.ds((c % 2) * (width // 2), width // 2)
        return hid.at[xi, j // per, pl.ds(pl.multiple_of(at, sr), sr), cols]

    for h in range(parts):
        mine[h].wait()
        for r in range(xn - 1):
            fo = 2 * ((x + r + 1) % xn) + k
            for j in range(h * per, (h + 1) * per):
                blk = rows(x, k, v, j)
                remote(blk, blk, x_send.at[r], recv.at[r, 0, j], v, fo).start()
        for r in range(xn - 1):
            fo = 2 * ((x + r + 1) % xn) + k
            for j in range(h * per + per // 2, (h + 1) * per):
                blk = rows(x, k, vd, j)
                remote(blk, blk, x_send.at[r], recv.at[r, 3, j], v, fo).start()
        remote(half(x, k, h), half(x, k, h), own_send, own_recv.at[h], v, sib).start()
    loads[5].start()

    def src_of(r):
        return (x + xn - r - 1) % xn

    owners = (v, vy, vz, vd)

    def arrive(r, rel, j):
        blk = rows(src_of(r), k, owners[rel], j)
        remote(blk, blk, x_send.at[r], recv.at[r, rel, j], v, f).wait_recv()
        relay = j % per < per // 2
        if rel == 0:
            remote(blk, blk, y_send.at[r], recv.at[r, 1, j], vy, f).start()
            remote(blk, blk, z_send.at[r], recv.at[r, 2, j], vz, f).start()
        if rel == 1 and relay and j % 2 == 0:
            remote(blk, blk, z_send.at[r], recv.at[r, 3, j], vz, f).start()
        if rel == 2 and relay and j % 2 == 1:
            remote(blk, blk, y_send.at[r], recv.at[r, 3, j], vy, f).start()
        remote(blk, blk, s_send.at[r], s_recv.at[r, j // per], v, sib).start()

    def post(send_buf, recv_buf, sem, d):
        @pl.when(d != me)
        def _():
            remote(send_buf, recv_buf, sem.at[0], sem.at[1], d // nf, d % nf).start()

    hear(1)
    loads[0].wait()
    loads[1].wait()
    o_t[...] = oproj[...].astype(F32).T.astype(BF16)
    base = me * vl

    def onehot_step(c, carry):
        xi, h = c // parts, c % parts
        blks = [(2 * xi + kk) * parts + h for kk in range(2)]
        ids = lax.broadcasted_iota(jnp.int32, (vl, tc), 0) + base
        goal = jnp.concatenate([targets[b] for b in blks], axis=1)
        hot = (goal == ids).astype(F32).astype(BF16)
        o = jnp.dot(o_t[...], hot, preferred_element_type=F32)
        o_full[c] = o
        for kk in range(2):
            for g in range(nf):
                so[g % 2, g // 2, blks[kk]] = o[g * rf:(g + 1) * rf, kk * tb:(kk + 1) * tb].astype(BF16)
        return carry

    with jax.named_scope("onehot"):
        lax.fori_loop(0, xn * parts, onehot_step, 0)
    over = remote(so.at[1 - k], r0, so_sem.at[0], so_sem.at[1], v, sib)
    over.start()

    def across(p, g):
        return remote(r0.at[g], r1.at[p - 1], ox_send.at[p - 1], ox_recv.at[p - 1], v, 2 * g + k)

    def onehot_over():
        over.wait_recv()

        def one(b, c):
            for g in range(xn):
                r0[g, b] = r0[g, b] + so[k, g, b]
            return c

        lax.fori_loop(0, nv, one, 0)
        for p in range(1, xn):
            across(p, (x + p) % xn).start()

    def spread_to(p):
        b = block((v + p) % nv)
        return remote(s2.at[b], ro.at[p - 1], ro_sem.at[0], ro_sem.at[1], (v + p) % nv, f)

    def onehot_sum():
        for p in range(1, xn):
            across(p, x).wait_recv()

        def one(b, c):
            t = r0[x, b]
            for p in range(1, xn):
                t = t + r1[p - 1, b]
            s2[b] = t
            return c

        lax.fori_loop(0, nv, one, 0)
        for p in range(1, nv):
            spread_to(p).start()

    def tiles(xi, h, lo, hi, m):
        vt = (hi - lo) // 2

        def tile(i, m):
            at = pl.ds(pl.multiple_of(i * vt, vt), vt)
            l = lax.dot_general(head[at, :], hid[xi, h], NT, preferred_element_type=F32)
            lg[at, :] = l
            return jnp.maximum(m, jnp.max(l, axis=0, keepdims=True))

        with jax.named_scope("tiles"):
            return lax.fori_loop(lo // vt, hi // vt, tile, m)

    def finish(xi, h, m):
        with jax.named_scope("finish"):
            e = jnp.exp(lg[...] - m)
            s = jnp.sum(e, axis=0, keepdims=True)
            u = jnp.dot(o_t[...], e.astype(BF16), preferred_element_type=F32)
            u = u / s - o_full[xi * parts + h]
            own = [owner(h, 2 * xi + kk) for kk in range(2)]
            for kk in range(2):
                lanes = slice(kk * tb, (kk + 1) * tb)
                st[own[kk], 0:1, :] = m[:, lanes]
                st[own[kk], 1:2, :] = s[:, lanes]
                for g in range(nf):
                    sv[own[kk] * nf + g] = u[g * rf:(g + 1) * rf, lanes].astype(BF16)

    def share_out(xi, h):
        for kk in range(2):
            w = owner(h, 2 * xi + kk)
            for g in range(nf):
                d = w * nf + g
                post(st.at[w], rst.at[me], st_sem, d)
                post(sv.at[d], rv.at[me], sv_sem, d)

    def project(xi, h):
        with jax.named_scope("act"):
            act = jnp.dot(hid[xi, h], iproj[...], preferred_element_type=F32)
            hi = act.astype(BF16)
            lo = (act - hi.astype(F32)).astype(BF16)
            both = jnp.concatenate([hi, lo], axis=1)
            for kk in range(2):
                ins[(2 * xi + kk) * parts + h] = both[kk * tb:(kk + 1) * tb]

    low = jnp.full((1, tc), -jnp.inf, F32)
    every = range(xn - 1)

    def sibling(h):
        blk = half(x, 1 - k, h)
        remote(blk, blk, own_send, own_recv.at[h], v, sib).wait_recv()

    def arrivals(*which):
        with jax.named_scope("arr"):
            for rel, j in which:
                for r in every:
                    arrive(r, rel, j)

    def passed(r, h):
        with jax.named_scope("passed"):
            blk = half(src_of(r), 1 - k, h)
            remote(blk, blk, s_send.at[r], s_recv.at[r, h], v, sib).wait_recv()

    mid = vl // 2
    hear(2)
    loads[2].wait()
    loads[3].wait()
    sibling(0)
    m = tiles(x, 0, 0, mid, low)
    hear(3)
    arrivals((0, 0))
    hear(4)
    m = tiles(x, 0, mid, vl, m)
    arrivals((0, 1))
    finish(x, 0, m)
    sibling(1)
    m = tiles(x, 1, 0, mid, low)
    arrivals((0, 2), (1, 0), (2, 0))
    with jax.named_scope("hear"):
        hear(len(near))
    arrivals((0, 3))
    m = tiles(x, 1, mid, vl, m)
    arrivals((1, 1), (2, 1), (3, 2))
    finish(x, 1, m)
    project(x, 0)
    arrivals((3, 3), (1, 2), (2, 2))
    with jax.named_scope("over"):
        onehot_over()
    arrivals((0, 4), (1, 3), (2, 3))
    project(x, 1)
    arrivals((0, 5), (3, 0), (3, 1), (0, 6))
    for r in every:
        passed(r, 0)
        m = tiles(src_of(r), 0, 0, mid, low)
        if r == 0:
            arrivals((0, 7), (1, 4), (2, 4), (1, 5), (2, 5))
        m = tiles(src_of(r), 0, mid, vl, m)
        if r == 0:
            arrivals((3, 6), (1, 6), (2, 6), (3, 7))
        finish(src_of(r), 0, m)
    with jax.named_scope("ohsum"):
        onehot_sum()
    arrivals((3, 4), (3, 5), (1, 7), (2, 7))
    share_out(x, 1)
    share_out(x, 0)
    for r in every:
        share_out(src_of(r), 0)
    for r in every:
        passed(r, 1)
        finish(src_of(r), 1, tiles(src_of(r), 1, 0, vl, low))
        share_out(src_of(r), 1)
    for r in every:
        project(src_of(r), 0)
        project(src_of(r), 1)

    local = [pltpu.make_async_copy(sv.at[me], rv.at[me], loc_sem.at[0]),
             pltpu.make_async_copy(st.at[v], rst.at[me], loc_sem.at[1])]
    for copy in local:
        copy.start()
    loads[4].wait()
    some = ro.at[pl.ds(0, nv - 1)]
    with jax.named_scope("row"):
        remote(some, some, ro_sem.at[0], ro_sem.at[1], v, f).wait_recv()
    targeted = s2[mb].astype(F32)
    for p in range(1, nv):
        targeted = targeted + ro[p - 1].astype(F32)
    for copy in local:
        copy.wait()
    stats, shares = rst.at[pl.ds(0, nd - 1)], rv.at[pl.ds(0, nd - 1)]
    with jax.named_scope("take"):
        remote(stats, stats, st_sem.at[0], st_sem.at[1], v, f).wait_recv()
        remote(shares, shares, sv_sem.at[0], sv_sem.at[1], v, f).wait_recv()
    peak, mass = rst[:, 0, :], rst[:, 1, :]
    mass = jnp.exp(peak - jnp.max(peak, axis=0, keepdims=True)) * mass
    share = mass / jnp.sum(mass, axis=0, keepdims=True)
    first_row = lax.broadcasted_iota(jnp.int32, (nd, tb), 0) * vl
    goal = targets[mb]
    outside = (goal < first_row) | (goal >= first_row + vl)
    acc = -jnp.sum(jnp.where(outside, share, 0.0), axis=0, keepdims=True) * targeted
    for d in range(nd):
        w = share[d:d + 1, :]
        acc = acc + w * rv[d].astype(F32)
    osb[mb] = acc

    with jax.named_scope("spread"):
        for p in range(1, nv):
            remote(osb.at[mb], osb.at[mb], ag_send, ag_recv.at[v], (v + p) % nv, f).start()

    def outer(first, b1, b2):
        for b in (b1, b2):
            w = owner(b % 2, b // 2)

            @pl.when(v != w)
            def _():
                with jax.named_scope("agw"):
                    remote(osb.at[b], osb.at[b], ag_send, ag_recv.at[w], v, f).wait_recv()

        with jax.named_scope("outer"):
            member = jnp.concatenate([seqs[b1], seqs[b2]], axis=1) == lax.broadcasted_iota(jnp.int32, (SEQS, tc), 0)
            member = member.astype(F32)
            o = jnp.concatenate([osb[b1], osb[b2]], axis=1)
            hi = o.astype(BF16).astype(F32)
            lo = o - hi
            w_hi = jnp.concatenate([(member * hi[i:i + 1, :]).astype(BF16) for i in range(rf)], axis=0)
            w_lo = jnp.concatenate([(member * lo[i:i + 1, :]).astype(BF16) for i in range(rf)], axis=0)
            right = jnp.concatenate([ins[b1], ins[b2]], axis=0)
            t = jnp.dot(w_hi, right, preferred_element_type=F32)
            t = t[:, :rank] + t[:, rank:] + jnp.dot(w_lo, right[:, :rank], preferred_element_type=F32)
            qg[...] = t if first else qg[...] + t

    for b in range(0, nv, 4):
        outer(b == 0, b, b + 2)
    for b in range(1, nv, 4):
        outer(False, b, b + 2)
    for i in range(rf):
        qgm[:, i * rank:(i + 1) * rank] = qg[i * SEQS:(i + 1) * SEQS, :].astype(BF16)
    loads[5].wait()

    def score(p, c):
        t = p + 1
        g = 2 * ((x + t // 2) % xn) + (k + 1 + t % 2) % 2
        part[g] = lax.dot_general(
            qgm[...], gs[pl.ds(pl.multiple_of(g * eo, eo), eo), :], NT, preferred_element_type=F32)

        @pl.when(p < nf)
        def _():
            remote(part.at[g], infl.at[p - 1], in_sem.at[0], in_sem.at[1], v, g).start()
        return c

    with jax.named_scope("score"):
        lax.fori_loop(1, nf + 1, score, 0)
    result = part[f]
    with jax.named_scope("inflw"):
        landed = infl.at[pl.ds(0, nf - 1)]
        remote(landed, landed, in_sem.at[0], in_sem.at[1], v, f).wait_recv()
    for p in range(1, nf):
        result = result + infl[p - 1]
    out[...] = result

    def sent(ref, sem):
        remote(ref, ref, sem, sem, v, f).wait_send()

    with jax.named_scope("drain"):
        chunk = sr // 2
        for r in every:
            sent(hid.at[0, 0, pl.ds(0, (SUBS + per) * chunk)], x_send.at[r])
            sent(hid.at[0, 0, pl.ds(0, (SUBS + per // 2) * chunk)], y_send.at[r])
            sent(hid.at[0, 0, pl.ds(0, (SUBS + per // 2) * chunk)], z_send.at[r])
            sent(hid.at[0, 0], s_send.at[r])
        sent(hid.at[0, 0], own_send)
        over.wait_send()
        for p in range(1, xn):
            across(p, x).wait_send()
        sent(some, ro_sem.at[0])
        sent(stats, st_sem.at[0])
        sent(shares, sv_sem.at[0])
        sent(osb.at[pl.ds(0, nv - 1)], ag_send)
        sent(landed, in_sem.at[0])


def solution(mesh):
    nv, nf = mesh.shape["vocab"], mesh.shape["feat"]
    nd = nv * nf
    xn = nf // 2

    def on_device(hidden, out_head, out_proj, in_proj, targets, seq_ids, grad_store):
        tl, width = hidden.shape
        vl, rank = out_proj.shape
        el, fl = grad_store.shape
        tokens = tl * nf
        rf, tb, eo = rank // nf, tokens // nv, el // nf
        parts = tl // tb
        any_spec = pl.BlockSpec(memory_space=pl.ANY)
        vmem = pl.BlockSpec(memory_space=pltpu.VMEM)
        dma = pltpu.SemaphoreType.DMA
        res = pl.pallas_call(
            functools.partial(kernel, nv, nf),
            out_shape=jax.ShapeDtypeStruct((SEQS, eo), F32),
            in_specs=[any_spec] * 7,
            out_specs=vmem,
            scratch_shapes=[
                pltpu.VMEM((xn, parts, 2 * tb, width), BF16),
                pltpu.VMEM((vl, width), BF16),
                pltpu.VMEM((vl, rank), BF16),
                pltpu.VMEM((width, rank), BF16),
                pltpu.VMEM((nv, 1, tb), jnp.int32),
                pltpu.VMEM((nv, 1, tb), jnp.int32),
                pltpu.VMEM((el, fl), BF16),
                pltpu.VMEM((vl, 2 * tb), F32),
                pltpu.VMEM((rank, vl), BF16),
                pltpu.VMEM((xn * parts, rank, 2 * tb), F32),
                pltpu.VMEM((nv, tb, 2 * rank), BF16),
                pltpu.VMEM((nd, rf, tb), BF16),
                pltpu.VMEM((2, xn, nv, rf, tb), BF16),
                pltpu.VMEM((nv, rf, tb), BF16),
                pltpu.VMEM((nv, 2, tb), F32),
                pltpu.VMEM((nd, rf, tb), BF16),
                pltpu.VMEM((xn, nv, rf, tb), BF16),
                pltpu.VMEM((xn - 1, nv, rf, tb), BF16),
                pltpu.VMEM((nv - 1, rf, tb), BF16),
                pltpu.VMEM((nd, 2, tb), F32),
                pltpu.VMEM((nv, rf, tb), F32),
                pltpu.VMEM((rf * SEQS, rank), F32),
                pltpu.VMEM((SEQS, fl), BF16),
                pltpu.VMEM((nf, SEQS, eo), F32),
                pltpu.VMEM((nf - 1, SEQS, eo), F32),
                dma((6 + parts,)),
                dma((xn - 1,)),
                dma((xn - 1,)),
                dma((xn - 1,)),
                dma((xn - 1,)),
                dma,
                dma((xn - 1, 4, SUBS)),
                dma((xn - 1, parts)),
                dma((parts,)),
                dma((2,)),
                dma((xn - 1,)),
                dma((xn - 1,)),
                dma((2,)),
                dma((2,)),
                dma((2,)),
                dma,
                dma((nv,)),
                dma((2,)),
                dma((2,)),
                pltpu.SemaphoreType.REGULAR((nf.bit_length() + nv.bit_length() - 2,)),
            ],
            compiler_params=pltpu.CompilerParams(
                collective_id=0, has_side_effects=True, vmem_limit_bytes=60 * 1024 * 1024),
        )(hidden, out_head, out_proj, in_proj, targets.reshape(nv, 1, tb), seq_ids.reshape(nv, 1, tb), grad_store)
        return res.T

    in_specs = (
        P("feat", None),
        P(("vocab", "feat"), None),
        P(("vocab", "feat"), None),
        P(),
        P(),
        P(),
        P("vocab", "feat"),
    )
    return jax.shard_map(
        on_device, mesh=mesh, in_specs=in_specs, out_specs=P(("vocab", "feat"), None), check_vma=False
    )
```

```python
import functools

import jax
import jax.numpy as jnp
from jax import lax
from jax.experimental import pallas as pl
from jax.experimental.pallas import tpu as pltpu
from jax.sharding import PartitionSpec as P

SEQS = 16
SUBS = 8
F32 = jnp.float32
BF16 = jnp.bfloat16
NT = (((1,), (1,)), ((), ()))


def kernel(nv, nf, hid_in, head_in, oproj_in, iproj_in, targets_in, seqs_in, gs_in, out,
           hid, head, oproj, iproj, targets, seqs, gs, lg, o_t, o_full, ins, sv, so, s2, st, rv, r0, r1, ro, rst, osb,
           qg, qgm, part, infl,
           load_sem, x_send, y_send, z_send, s_send, own_send, recv, s_recv, own_recv, so_sem, ox_send, ox_recv, ro_sem,
           sv_sem, st_sem, ag_send, ag_recv, in_sem, loc_sem, heard):
    v = lax.axis_index("vocab")
    f = lax.axis_index("feat")
    me = v * nf + f
    nd = nv * nf
    x, k = f // 2, f % 2
    xn = nf // 2
    sib = f + 1 - 2 * k
    vy = v + 1 - 2 * (v % 2)
    vz = v + 2 - 4 * ((v // 2) % 2)
    vd = vy + vz - v
    vl = head.shape[0]
    width = head.shape[1]
    rank = oproj.shape[1]
    rf, tb = sv.shape[1], sv.shape[2]
    parts = hid.shape[1]
    tc = 2 * tb
    eo = out.shape[1]
    piece = tb // 4
    per = SUBS // parts
    sr = 2 * piece // per
    quarter = nv // 4

    def owner(h, i):
        spot = (1 - i % 2) * (i // 2) + (i % 2) * (2 * quarter - 1 - i // 2)
        return quarter + spot if h else spot + 2 * quarter * (spot // quarter)

    def block(w):
        late = ((w // quarter + 1) // 2) % 2
        spot = late * (w - quarter) + (1 - late) * (w - 2 * quarter * (w // (2 * quarter)))
        i = (1 - spot // quarter) * 2 * spot + (spot // quarter) * (4 * quarter - 1 - 2 * spot)
        return 2 * i + late

    mb = block(v)

    loads = [
        pltpu.make_async_copy(oproj_in, oproj, load_sem.at[0]),
        pltpu.make_async_copy(targets_in, targets, load_sem.at[1]),
        pltpu.make_async_copy(head_in, head, load_sem.at[2]),
        pltpu.make_async_copy(iproj_in, iproj, load_sem.at[3]),
        pltpu.make_async_copy(seqs_in, seqs, load_sem.at[4]),
        pltpu.make_async_copy(gs_in, gs, load_sem.at[5]),
    ]

    def half(xi, kk, h):
        return hid.at[xi, h, pl.ds(pl.multiple_of(kk * tb, tb), tb)]

    mine = [pltpu.make_async_copy(hid_in.at[pl.ds(h * tb, tb)], half(x, k, h), load_sem.at[6 + h])
            for h in range(parts)]

    def flip(i, bit):
        return i + bit - 2 * bit * ((i // bit) % 2)

    near = [(v, flip(f, 1 << i)) for i in range(nf.bit_length() - 1)]
    near += [(flip(v, 1 << i), f) for i in range(nv.bit_length() - 1)]
    barrier = pltpu.get_barrier_semaphore()

    def signal(sem, place):
        pl.semaphore_signal(sem, inc=1, device_id={"vocab": place[0], "feat": place[1]},
                            device_id_type=pl.DeviceIdType.MESH)

    for place in near:
        signal(barrier, place)
    for copy in mine + loads[:5]:
        copy.start()
    with jax.named_scope("barrier"):
        pl.semaphore_wait(barrier, len(near))
    said = [0]

    def hear(upto):
        for i in range(said[0], upto):
            pl.semaphore_wait(heard.at[i], 1)
            if i + 1 < len(near):
                signal(heard.at[i + 1], near[i + 1])
        said[0] = max(said[0], upto)

    signal(heard.at[0], near[0])
    if xn > 2:
        hear(nf.bit_length() - 1)

    def remote(src, dst, ss, rs, dv, df):
        return pltpu.make_async_remote_copy(
            src_ref=src, dst_ref=dst, send_sem=ss, recv_sem=rs,
            device_id={"vocab": dv, "feat": df}, device_id_type=pl.DeviceIdType.MESH)

    def rows(xi, kk, own, j):
        c = j % per
        at = kk * tb + (own % 4) * piece + (c // 2) * sr
        cols = pl.ds((c % 2) * (width // 2), width // 2)
        return hid.at[xi, j // per, pl.ds(pl.multiple_of(at, sr), sr), cols]

    for h in range(parts):
        mine[h].wait()
        for r in range(xn - 1):
            fo = 2 * ((x + r + 1) % xn) + k
            for j in range(h * per, (h + 1) * per):
                blk = rows(x, k, v, j)
                remote(blk, blk, x_send.at[r], recv.at[r, 0, j], v, fo).start()
        for r in range(xn - 1):
            fo = 2 * ((x + r + 1) % xn) + k
            for j in range(h * per + per // 2, (h + 1) * per):
                blk = rows(x, k, vd, j)
                remote(blk, blk, x_send.at[r], recv.at[r, 3, j], v, fo).start()
        remote(half(x, k, h), half(x, k, h), own_send, own_recv.at[h], v, sib).start()
    loads[5].start()

    def src_of(r):
        return (x + xn - r - 1) % xn

    owners = (v, vy, vz, vd)

    def arrive(r, rel, j):
        blk = rows(src_of(r), k, owners[rel], j)
        remote(blk, blk, x_send.at[r], recv.at[r, rel, j], v, f).wait_recv()
        relay = j % per < per // 2
        if rel == 0:
            remote(blk, blk, y_send.at[r], recv.at[r, 1, j], vy, f).start()
            remote(blk, blk, z_send.at[r], recv.at[r, 2, j], vz, f).start()
        if rel == 1 and relay and j % 2 == 0:
            remote(blk, blk, z_send.at[r], recv.at[r, 3, j], vz, f).start()
        if rel == 2 and relay and j % 2 == 1:
            remote(blk, blk, y_send.at[r], recv.at[r, 3, j], vy, f).start()
        remote(blk, blk, s_send.at[r], s_recv.at[r, j // per], v, sib).start()

    def post(send_buf, recv_buf, sem, d):
        @pl.when(d != me)
        def _():
            remote(send_buf, recv_buf, sem.at[0], sem.at[1], d // nf, d % nf).start()

    hear(1)
    loads[0].wait()
    loads[1].wait()
    o_t[...] = oproj[...].astype(F32).T.astype(BF16)
    base = me * vl

    def onehot_step(c, carry):
        xi, h = c // parts, c % parts
        blks = [(2 * xi + kk) * parts + h for kk in range(2)]
        ids = lax.broadcasted_iota(jnp.int32, (vl, tc), 0) + base
        goal = jnp.concatenate([targets[b] for b in blks], axis=1)
        hot = (goal == ids).astype(F32).astype(BF16)
        o = jnp.dot(o_t[...], hot, preferred_element_type=F32)
        o_full[c] = o
        for kk in range(2):
            for g in range(nf):
                so[g % 2, g // 2, blks[kk]] = o[g * rf:(g + 1) * rf, kk * tb:(kk + 1) * tb].astype(BF16)
        return carry

    with jax.named_scope("onehot"):
        lax.fori_loop(0, xn * parts, onehot_step, 0)
    over = remote(so.at[1 - k], r0, so_sem.at[0], so_sem.at[1], v, sib)
    over.start()

    def across(p, g):
        return remote(r0.at[g], r1.at[p - 1], ox_send.at[p - 1], ox_recv.at[p - 1], v, 2 * g + k)

    def onehot_over():
        over.wait_recv()

        def one(b, c):
            for g in range(xn):
                r0[g, b] = r0[g, b] + so[k, g, b]
            return c

        lax.fori_loop(0, nv, one, 0)
        for p in range(1, xn):
            across(p, (x + p) % xn).start()

    def spread_to(p):
        b = block((v + p) % nv)
        return remote(s2.at[b], ro.at[p - 1], ro_sem.at[0], ro_sem.at[1], (v + p) % nv, f)

    def onehot_sum():
        for p in range(1, xn):
            across(p, x).wait_recv()

        def one(b, c):
            t = r0[x, b]
            for p in range(1, xn):
                t = t + r1[p - 1, b]
            s2[b] = t
            return c

        lax.fori_loop(0, nv, one, 0)
        for p in range(1, nv):
            spread_to(p).start()

    def tiles(xi, h, lo, hi, m):
        vt = (hi - lo) // 2

        def tile(i, m):
            at = pl.ds(pl.multiple_of(i * vt, vt), vt)
            l = lax.dot_general(head[at, :], hid[xi, h], NT, preferred_element_type=F32)
            lg[at, :] = l
            return jnp.maximum(m, jnp.max(l, axis=0, keepdims=True))

        with jax.named_scope("tiles"):
            return lax.fori_loop(lo // vt, hi // vt, tile, m)

    def finish(xi, h, m):
        with jax.named_scope("finish"):
            e = jnp.exp(lg[...] - m)
            s = jnp.sum(e, axis=0, keepdims=True)
            u = jnp.dot(o_t[...], e.astype(BF16), preferred_element_type=F32)
            u = u / s - o_full[xi * parts + h]
            own = [owner(h, 2 * xi + kk) for kk in range(2)]
            for kk in range(2):
                lanes = slice(kk * tb, (kk + 1) * tb)
                st[own[kk], 0:1, :] = m[:, lanes]
                st[own[kk], 1:2, :] = s[:, lanes]
                for g in range(nf):
                    sv[own[kk] * nf + g] = u[g * rf:(g + 1) * rf, lanes].astype(BF16)

    def share_out(xi, h):
        for kk in range(2):
            w = owner(h, 2 * xi + kk)
            for g in range(nf):
                d = w * nf + g
                post(st.at[w], rst.at[me], st_sem, d)
                post(sv.at[d], rv.at[me], sv_sem, d)

    def project(xi, h):
        with jax.named_scope("act"):
            act = jnp.dot(hid[xi, h], iproj[...], preferred_element_type=F32)
            hi = act.astype(BF16)
            lo = (act - hi.astype(F32)).astype(BF16)
            both = jnp.concatenate([hi, lo], axis=1)
            for kk in range(2):
                ins[(2 * xi + kk) * parts + h] = both[kk * tb:(kk + 1) * tb]

    low = jnp.full((1, tc), -jnp.inf, F32)
    every = range(xn - 1)

    def sibling(h):
        blk = half(x, 1 - k, h)
        remote(blk, blk, own_send, own_recv.at[h], v, sib).wait_recv()

    def arrivals(*which):
        with jax.named_scope("arr"):
            for rel, j in which:
                for r in every:
                    arrive(r, rel, j)

    def passed(r, h):
        with jax.named_scope("passed"):
            blk = half(src_of(r), 1 - k, h)
            remote(blk, blk, s_send.at[r], s_recv.at[r, h], v, sib).wait_recv()

    mid = vl // 2
    hear(2)
    loads[2].wait()
    loads[3].wait()
    sibling(0)
    m = tiles(x, 0, 0, mid, low)
    hear(3)
    arrivals((0, 0))
    hear(4)
    m = tiles(x, 0, mid, vl, m)
    arrivals((0, 1))
    finish(x, 0, m)
    sibling(1)
    m = tiles(x, 1, 0, mid, low)
    arrivals((0, 2), (1, 0), (2, 0))
    with jax.named_scope("hear"):
        hear(len(near))
    arrivals((0, 3))
    m = tiles(x, 1, mid, vl, m)
    arrivals((1, 1), (2, 1), (3, 2))
    finish(x, 1, m)
    project(x, 0)
    arrivals((3, 3), (1, 2), (2, 2))
    with jax.named_scope("over"):
        onehot_over()
    arrivals((0, 4), (1, 3), (2, 3), (0, 5), (3, 0), (3, 1), (0, 6), (1, 4), (2, 4))
    for r in every:
        passed(r, 0)
        m = tiles(src_of(r), 0, 0, mid, low)
        if r == 0:
            arrivals((0, 7))
        m = tiles(src_of(r), 0, mid, vl, m)
        if r == 0:
            arrivals((1, 5), (2, 5))
        finish(src_of(r), 0, m)
    with jax.named_scope("ohsum"):
        onehot_sum()
    arrivals((3, 6), (1, 6), (2, 6))
    project(x, 1)
    arrivals((3, 7), (3, 4), (3, 5), (1, 7), (2, 7))
    share_out(x, 0)
    for r in every:
        share_out(src_of(r), 0)
    share_out(x, 1)
    for r in every:
        passed(r, 1)
        finish(src_of(r), 1, tiles(src_of(r), 1, 0, vl, low))
        share_out(src_of(r), 1)
    for r in every:
        project(src_of(r), 0)
        project(src_of(r), 1)

    local = [pltpu.make_async_copy(sv.at[me], rv.at[me], loc_sem.at[0]),
             pltpu.make_async_copy(st.at[v], rst.at[me], loc_sem.at[1])]
    for copy in local:
        copy.start()
    loads[4].wait()
    some = ro.at[pl.ds(0, nv - 1)]
    with jax.named_scope("row"):
        remote(some, some, ro_sem.at[0], ro_sem.at[1], v, f).wait_recv()
    targeted = s2[mb].astype(F32)
    for p in range(1, nv):
        targeted = targeted + ro[p - 1].astype(F32)
    for copy in local:
        copy.wait()
    stats, shares = rst.at[pl.ds(0, nd - 1)], rv.at[pl.ds(0, nd - 1)]
    with jax.named_scope("take"):
        remote(stats, stats, st_sem.at[0], st_sem.at[1], v, f).wait_recv()
        remote(shares, shares, sv_sem.at[0], sv_sem.at[1], v, f).wait_recv()
    peak, mass = rst[:, 0, :], rst[:, 1, :]
    mass = jnp.exp(peak - jnp.max(peak, axis=0, keepdims=True)) * mass
    share = mass / jnp.sum(mass, axis=0, keepdims=True)
    first_row = lax.broadcasted_iota(jnp.int32, (nd, tb), 0) * vl
    goal = targets[mb]
    outside = (goal < first_row) | (goal >= first_row + vl)
    acc = -jnp.sum(jnp.where(outside, share, 0.0), axis=0, keepdims=True) * targeted
    for d in range(nd):
        w = share[d:d + 1, :]
        acc = acc + w * rv[d].astype(F32)
    osb[mb] = acc

    with jax.named_scope("spread"):
        for p in range(1, nv):
            remote(osb.at[mb], osb.at[mb], ag_send, ag_recv.at[v], (v + p) % nv, f).start()

    def outer(first, b1, b2):
        for b in (b1, b2):
            w = owner(b % 2, b // 2)

            @pl.when(v != w)
            def _():
                with jax.named_scope("agw"):
                    remote(osb.at[b], osb.at[b], ag_send, ag_recv.at[w], v, f).wait_recv()

        with jax.named_scope("outer"):
            member = jnp.concatenate([seqs[b1], seqs[b2]], axis=1) == lax.broadcasted_iota(jnp.int32, (SEQS, tc), 0)
            member = member.astype(F32)
            o = jnp.concatenate([osb[b1], osb[b2]], axis=1)
            hi = o.astype(BF16).astype(F32)
            lo = o - hi
            w_hi = jnp.concatenate([(member * hi[i:i + 1, :]).astype(BF16) for i in range(rf)], axis=0)
            w_lo = jnp.concatenate([(member * lo[i:i + 1, :]).astype(BF16) for i in range(rf)], axis=0)
            right = jnp.concatenate([ins[b1], ins[b2]], axis=0)
            t = jnp.dot(w_hi, right, preferred_element_type=F32)
            t = t[:, :rank] + t[:, rank:] + jnp.dot(w_lo, right[:, :rank], preferred_element_type=F32)
            qg[...] = t if first else qg[...] + t

    for b in range(0, nv, 4):
        outer(b == 0, b, b + 2)
    for b in range(1, nv, 4):
        outer(False, b, b + 2)
    for i in range(rf):
        qgm[:, i * rank:(i + 1) * rank] = qg[i * SEQS:(i + 1) * SEQS, :].astype(BF16)
    loads[5].wait()

    def score(p, c):
        t = p + 1
        g = 2 * ((x + t // 2) % xn) + (k + 1 + t % 2) % 2
        part[g] = lax.dot_general(
            qgm[...], gs[pl.ds(pl.multiple_of(g * eo, eo), eo), :], NT, preferred_element_type=F32)

        @pl.when(p < nf)
        def _():
            remote(part.at[g], infl.at[p - 1], in_sem.at[0], in_sem.at[1], v, g).start()
        return c

    with jax.named_scope("score"):
        lax.fori_loop(1, nf + 1, score, 0)
    result = part[f]
    with jax.named_scope("inflw"):
        landed = infl.at[pl.ds(0, nf - 1)]
        remote(landed, landed, in_sem.at[0], in_sem.at[1], v, f).wait_recv()
    for p in range(1, nf):
        result = result + infl[p - 1]
    out[...] = result

    def sent(ref, sem):
        remote(ref, ref, sem, sem, v, f).wait_send()

    with jax.named_scope("drain"):
        chunk = sr // 2
        for r in every:
            sent(hid.at[0, 0, pl.ds(0, (SUBS + per) * chunk)], x_send.at[r])
            sent(hid.at[0, 0, pl.ds(0, (SUBS + per // 2) * chunk)], y_send.at[r])
            sent(hid.at[0, 0, pl.ds(0, (SUBS + per // 2) * chunk)], z_send.at[r])
            sent(hid.at[0, 0], s_send.at[r])
        sent(hid.at[0, 0], own_send)
        over.wait_send()
        for p in range(1, xn):
            across(p, x).wait_send()
        sent(some, ro_sem.at[0])
        sent(stats, st_sem.at[0])
        sent(shares, sv_sem.at[0])
        sent(osb.at[pl.ds(0, nv - 1)], ag_send)
        sent(landed, in_sem.at[0])


def solution(mesh):
    nv, nf = mesh.shape["vocab"], mesh.shape["feat"]
    nd = nv * nf
    xn = nf // 2

    def on_device(hidden, out_head, out_proj, in_proj, targets, seq_ids, grad_store):
        tl, width = hidden.shape
        vl, rank = out_proj.shape
        el, fl = grad_store.shape
        tokens = tl * nf
        rf, tb, eo = rank // nf, tokens // nv, el // nf
        parts = tl // tb
        any_spec = pl.BlockSpec(memory_space=pl.ANY)
        vmem = pl.BlockSpec(memory_space=pltpu.VMEM)
        dma = pltpu.SemaphoreType.DMA
        res = pl.pallas_call(
            functools.partial(kernel, nv, nf),
            out_shape=jax.ShapeDtypeStruct((SEQS, eo), F32),
            in_specs=[any_spec] * 7,
            out_specs=vmem,
            scratch_shapes=[
                pltpu.VMEM((xn, parts, 2 * tb, width), BF16),
                pltpu.VMEM((vl, width), BF16),
                pltpu.VMEM((vl, rank), BF16),
                pltpu.VMEM((width, rank), BF16),
                pltpu.VMEM((nv, 1, tb), jnp.int32),
                pltpu.VMEM((nv, 1, tb), jnp.int32),
                pltpu.VMEM((el, fl), BF16),
                pltpu.VMEM((vl, 2 * tb), F32),
                pltpu.VMEM((rank, vl), BF16),
                pltpu.VMEM((xn * parts, rank, 2 * tb), F32),
                pltpu.VMEM((nv, tb, 2 * rank), BF16),
                pltpu.VMEM((nd, rf, tb), BF16),
                pltpu.VMEM((2, xn, nv, rf, tb), BF16),
                pltpu.VMEM((nv, rf, tb), BF16),
                pltpu.VMEM((nv, 2, tb), F32),
                pltpu.VMEM((nd, rf, tb), BF16),
                pltpu.VMEM((xn, nv, rf, tb), BF16),
                pltpu.VMEM((xn - 1, nv, rf, tb), BF16),
                pltpu.VMEM((nv - 1, rf, tb), BF16),
                pltpu.VMEM((nd, 2, tb), F32),
                pltpu.VMEM((nv, rf, tb), F32),
                pltpu.VMEM((rf * SEQS, rank), F32),
                pltpu.VMEM((SEQS, fl), BF16),
                pltpu.VMEM((nf, SEQS, eo), F32),
                pltpu.VMEM((nf - 1, SEQS, eo), F32),
                dma((6 + parts,)),
                dma((xn - 1,)),
                dma((xn - 1,)),
                dma((xn - 1,)),
                dma((xn - 1,)),
                dma,
                dma((xn - 1, 4, SUBS)),
                dma((xn - 1, parts)),
                dma((parts,)),
                dma((2,)),
                dma((xn - 1,)),
                dma((xn - 1,)),
                dma((2,)),
                dma((2,)),
                dma((2,)),
                dma,
                dma((nv,)),
                dma((2,)),
                dma((2,)),
                pltpu.SemaphoreType.REGULAR((nf.bit_length() + nv.bit_length() - 2,)),
            ],
            compiler_params=pltpu.CompilerParams(
                collective_id=0, has_side_effects=True, vmem_limit_bytes=60 * 1024 * 1024),
        )(hidden, out_head, out_proj, in_proj, targets.reshape(nv, 1, tb), seq_ids.reshape(nv, 1, tb), grad_store)
        return res.T

    in_specs = (
        P("feat", None),
        P(("vocab", "feat"), None),
        P(("vocab", "feat"), None),
        P(),
        P(),
        P(),
        P("vocab", "feat"),
    )
    return jax.shard_map(
        on_device, mesh=mesh, in_specs=in_specs, out_specs=P(("vocab", "feat"), None), check_vma=False
    )
```
